32 devices in a mesh: parts: 2 (over y), seq: 4 (over z), head: 4 (over x, core).
Axes of the slice: x: 2, y: 2, z: 4, core: 2. Of those that a mesh axis runs over, the one named last changes fastest.
Arguments:
- queries: bfloat16 [256, 8192], P(('parts', 'seq'), 'head'), parts along dimension 0, may hold values from -110 to 110
- root_keys: bfloat16 [16384, 1024], P(('parts', 'seq'), 'head'), parts along dimension 0, may hold values from -6 to 6
- root_values: bfloat16 [16384, 1024], P(('parts', 'seq'), 'head'), parts along dimension 0, may hold values from -6 to 6
- branch_keys: bfloat16 [16, 2048, 1024], P(('parts', 'seq'), None, 'head'), parts along dimension 0, may hold values from -6 to 6
- branch_values: bfloat16 [16, 2048, 1024], P(('parts', 'seq'), None, 'head'), parts along dimension 0, may hold values from -6 to 6
- branch_id: int32 [256, 1], P('parts'), parts along dimension 0, may hold values from 0 to 7; in each aligned block of 128 rows (0 to 127, 128 to 255, ...) at most 32 rows name the same one
- doc_len: int32 [16], P('parts'), parts along dimension 0, may hold values from 1 to 2048, 10240 in all
Outputs:
- attended: bfloat16 [256, 8192], P(('parts', 'seq'), 'head'), parts along dimension 0
The draws below stay inside these ranges and needn't reach their ends.
There are 2 independent parts, one for each index of `parts`. The reference program is written for one: setup_inputs(seed, part) draws one part's arguments, and reference() takes and returns one part's arrays. A program takes and returns all parts, laid end to end along the dimension named above; each array names one. Nothing has to cross between parts.
Inputs may be any that keep to these rules, and one draw needn't show every extreme that they name: `branch_id`: each of the 8 branches is named by at most 32 rows, a bound that some block reaches. `doc_len`: the 8 lengths of ONE part sum to 10240 and the largest of them is exactly 2048; the printed array holds all parts end to end, so its whole sum is that total times the number of parts.
All inputs are finite; a program needn't handle non-finite values.
Results may differ from the reference program's by a relative error of at most 0.008.
Values may be sent and summed in bfloat16 or wider, within the bound.
A program may use at most 64 MiB of HBM per device.

```python
import math
import jax
import jax.numpy as jnp
import numpy as np
from jax import lax

QHEADS = 64
KVHEADS = 8
HEAD_DIM = 128
BRANCH_LEN = 2048
ROOT = 8192
ROWS = 128
BRANCHES = 8
MOST_ROWS = 32


def draw_queries(key, part):
    extent = (ROWS, QHEADS * HEAD_DIM)
    result = jnp.clip(jax.random.normal(key, extent, jnp.float32), -6.0, 6.0)
    return result.astype(jnp.bfloat16)


def shard_levels(stream_key, dims, cuts, low, high):
    loudness = 1.0
    for axis_at, blocks in cuts:
        steps = jax.random.uniform(jax.random.fold_in(jax.random.fold_in(stream_key, 6), axis_at), (blocks,), jnp.float32, low / len(cuts), high / len(cuts))
        loudness = loudness * jnp.repeat(jnp.exp(steps), dims[axis_at] // blocks).reshape((-1,) + (1,) * (len(dims) - 1 - axis_at))
    return loudness


def profile(amount, total, limit, skew):
    weights = [(1 << 20) // math.isqrt(standing ** skew) + 1 for standing in range(2, amount + 1)]
    surplus, given = total - limit - (amount - 1), [1] * (amount - 1)
    while surplus > 0:
        movable = [i for i in range(amount - 1) if given[i] < limit]
        mass, left = sum([weights[i] for i in movable]), surplus
        for i in movable:
            extra = min(limit - given[i], max(1, left * weights[i] // mass), surplus)
            given[i] = given[i] + extra
            surplus = surplus - extra
    return np.array([limit] + given)


def ragged(rng, amount, total, reach, skew):
    if amount == 2:
        one = jax.random.randint(rng, (), max(1, total - reach), min(reach, total - 1) + 1)
        return jnp.stack([one, total - one])
    tallies = jnp.asarray(profile(amount, total, reach, skew), jnp.int32)
    twos = (amount - 1) // 2
    giver, sink = tallies[1:1 + 2 * twos:2], tallies[2:2 + 2 * twos:2]
    slack = jnp.minimum(giver - 1, reach - sink)
    shifted = jax.random.randint(jax.random.fold_in(rng, 1), (twos,), 0, 1 << 20) % (slack + 1)
    tallies = tallies.at[1:1 + 2 * twos:2].set(giver - shifted).at[2:2 + 2 * twos:2].set(sink + shifted)
    return tallies[jax.random.permutation(jax.random.fold_in(rng, 2), amount)]


def assign_block(stream_key, own, number, rows, number_of, top, most, slope):
    sequence = jax.random.permutation(stream_key, number_of)
    heavy_load, ordinary = portions_of(number_of, rows * top, most, slope, True), portions_of(number_of, rows * top, most, slope, False)
    places = jnp.arange(number_of)

    def named(sizes, rotation):
        used = int((sizes > 0).sum())
        fixed = max(1, used // 4)
        shifted = fixed + (places - fixed + rotation * (used - fixed)) % max(1, number_of - fixed)
        return jnp.zeros((number_of,), jnp.int32).at[sequence[jnp.where(places < fixed, places, shifted)]].set(jnp.asarray(sizes, jnp.int32))

    sizes = jnp.where(number % 4 == 0, named(heavy_load, number // 4), named(ordinary, number - number // 4 - 1))
    mixed = jax.random.permutation(jax.random.fold_in(own, 3), number_of)
    giver, receiver = mixed[0:number_of // 2 * 2:2], mixed[1:number_of // 2 * 2:2]
    room = jnp.minimum(sizes[giver] - 1, most - sizes[receiver]) // 2
    room = jnp.where((giver == sequence[0]) | (receiver == sequence[0]) | (sizes[receiver] == 0), 0, jnp.maximum(room, 0))
    shifted = jax.random.randint(jax.random.fold_in(own, 4), (number_of // 2,), 0, 1 << 20) % (room + 1)
    sizes = sizes.at[giver].add(-shifted).at[receiver].add(shifted)
    members = jnp.searchsorted(jnp.cumsum(sizes), jnp.arange(rows * top), side="right").astype(jnp.int32)
    grid = members.reshape(top, rows).T
    grid = grid[jax.random.permutation(jax.random.fold_in(own, 1), rows)]
    rotation = jax.random.randint(jax.random.fold_in(own, 2), (rows, 1), 0, top)
    return jnp.take_along_axis(grid, (jnp.arange(top)[None, :] + rotation) % top, axis=1)


def portions_of(amount, total, reach, lean, full):
    portions = [(1 << 20) // math.isqrt(grade ** lean) + 1 for grade in range(1, amount + 1)]
    largest = reach if full else min(reach, max(-(-total // amount), total * portions[0] // sum(portions)))
    least = 1 if total - largest >= amount - 1 else 0
    given, surplus = [largest] + [least] * (amount - 1), total - largest - least * (amount - 1)
    while surplus > 0:
        movable = [i for i in range(1, amount) if given[i] < largest] or [i for i in range(1, amount) if given[i] < reach]
        mass, budget = sum([portions[i] for i in movable]), surplus
        for i in movable:
            extra = min(reach - given[i], max(1, budget * portions[i] // mass), surplus)
            given[i] = given[i] + extra
            surplus = surplus - extra
    return np.array(given)


def centred(rng, dims, scale, reach, cuts=(), kind=jnp.bfloat16):
    level = shard_levels(rng, dims, cuts, -0.22, 0.18) if cuts else 1.0
    values = jax.random.normal(rng, dims, jnp.float32) * scale * level
    return jnp.minimum(jnp.maximum(values, -reach), reach).astype(kind)


def setup_inputs(seed: int = 0, part: int = 0) -> dict:
    keys = jax.random.split(jax.random.key(seed), 8)
    part_keys = jax.random.split(jax.random.fold_in(keys[7], part), 8)
    queries = draw_queries(jax.random.fold_in(jax.random.fold_in(keys[7], part), 71), part)
    root_keys = centred(part_keys[1], (ROOT, KVHEADS * HEAD_DIM), 1.0, 6.0, ((0, 4), (1, 4)))
    root_values = centred(part_keys[2], (ROOT, KVHEADS * HEAD_DIM), 1.0, 6.0, ((0, 4), (1, 4)))
    branch_keys = centred(part_keys[3], (BRANCHES, BRANCH_LEN, KVHEADS * HEAD_DIM), 1.0, 6.0, ((0, 4), (2, 4)))
    branch_values = centred(part_keys[4], (BRANCHES, BRANCH_LEN, KVHEADS * HEAD_DIM), 1.0, 6.0, ((0, 4), (2, 4)))
    branch_id_keys = jax.random.split(jax.random.fold_in(part_keys[5], 1), ROWS // ROWS)
    branch_id_turns = jax.random.permutation(jax.random.fold_in(part_keys[5], 3), ROWS // ROWS)
    branch_id = jax.vmap(lambda own, number: assign_block(jax.random.fold_in(part_keys[5], 2), own, number, ROWS, BRANCHES, 1, MOST_ROWS, 2))(branch_id_keys, branch_id_turns).reshape((ROWS, 1))
    doc_len = ragged(part_keys[6], BRANCHES, BRANCHES * BRANCH_LEN * 5 // 8, BRANCH_LEN, 2).astype(jnp.int32)
    return {"queries": queries, "root_keys": root_keys, "root_values": root_values, "branch_keys": branch_keys, "branch_values": branch_values, "branch_id": branch_id, "doc_len": doc_len}


masked_score = -1.0e30


def attend(query_head_rows, key_tile_rows, value_tile_rows, usable):
    logit_scale = HEAD_DIM ** -0.5
    logit_scores = jnp.einsum('mfsa,nfa->mfsn', query_head_rows.astype(jnp.float32), key_tile_rows.astype(jnp.float32)) * logit_scale
    keep = usable[:, None, None, :]
    logit_scores = jnp.where(keep, logit_scores, masked_score)
    row_max = jnp.max(logit_scores, axis=-1)
    softmax_weights = jnp.where(keep, jnp.exp(logit_scores - row_max[..., None]), 0.0)
    row_sum = jnp.sum(softmax_weights, axis=-1)
    weighted_values = jnp.einsum('taoz,zah->taoh', softmax_weights.astype(jnp.bfloat16).astype(jnp.float32), value_tile_rows.astype(jnp.float32))
    return row_max, row_sum, weighted_values


def combine(first, second):
    row_max = jnp.maximum(first[0], second[0])
    factor_a = jnp.exp(first[0] - row_max)
    factor_b = jnp.exp(second[0] - row_max)
    return (row_max, first[1] * factor_a + second[1] * factor_b,
            first[2] * factor_a[..., None] + second[2] * factor_b[..., None])


def reference(queries, root_keys, root_values, branch_keys, branch_values, branch_id, doc_len):
    group = QHEADS // KVHEADS
    query_head_rows = queries.reshape(ROWS, KVHEADS, group, HEAD_DIM)
    block_len = min(1024, ROOT)
    key_blocks = root_keys.reshape(ROOT // block_len, block_len, KVHEADS, HEAD_DIM)
    value_blocks = root_values.reshape(ROOT // block_len, block_len, KVHEADS, HEAD_DIM)
    starts = (jnp.full((ROWS, KVHEADS, group), masked_score, jnp.float32),
              jnp.zeros((ROWS, KVHEADS, group), jnp.float32),
              jnp.zeros((ROWS, KVHEADS, group, HEAD_DIM), jnp.float32))

    def root_step(carry, pair):
        usable = jnp.ones((1, block_len), bool)
        return combine(carry, attend(query_head_rows, pair[0], pair[1], usable)), None

    root_part, _ = lax.scan(root_step, starts, (key_blocks, value_blocks))

    def one_branch(branch):
        chosen = jnp.argsort((branch_id[:, 0] != branch).astype(jnp.int32), stable=True)[:MOST_ROWS].astype(jnp.int32)
        row_live = branch_id[chosen, 0] == branch
        key_live = jnp.arange(BRANCH_LEN) < doc_len[branch]
        usable = row_live[:, None] & key_live[None, :]
        key_tile_rows = lax.dynamic_index_in_dim(branch_keys, branch, 0, keepdims=False).reshape(BRANCH_LEN, KVHEADS, HEAD_DIM)
        value_tile_rows = lax.dynamic_index_in_dim(branch_values, branch, 0, keepdims=False).reshape(BRANCH_LEN, KVHEADS, HEAD_DIM)
        result = attend(query_head_rows[chosen], key_tile_rows, value_tile_rows, usable)
        target = jnp.where(row_live, chosen, ROWS).astype(jnp.int32)
        return result + (target,)

    mapped = lax.map(one_branch, jnp.arange(BRANCHES, dtype=jnp.int32))
    targets = mapped[3].reshape(-1)
    branch_part = (
        starts[0].at[targets].set(mapped[0].reshape(-1, KVHEADS, group), mode="drop"),
        starts[1].at[targets].set(mapped[1].reshape(-1, KVHEADS, group), mode="drop"),
        starts[2].at[targets].set(mapped[2].reshape(-1, KVHEADS, group, HEAD_DIM), mode="drop"))
    joined = combine(root_part, branch_part)
    attended = joined[2] / joined[1][..., None]
    return attended.astype(jnp.bfloat16).reshape(ROWS, QHEADS * HEAD_DIM)
```

```python
import functools

import jax
import jax.numpy as jnp
from jax import lax
from jax.experimental import pallas as pl
from jax.experimental.pallas import tpu as pltpu
from jax.sharding import PartitionSpec as P

QHEADS = 64
KVHEADS = 8
HEAD_DIM = 128
GROUP = QHEADS // KVHEADS
MESH = pl.DeviceIdType.MESH
LOG2E = 1.4426950408889634
SCALE2 = HEAD_DIM ** (-0.5) * LOG2E
MASKED = -1e30
KEY_BLOCK = 512
CUT = 1
REACH = 1
SHARDS = 3


def attend(q, keys, values, live=None):
    size = min(KEY_BLOCK, keys.shape[0])
    blocks = [slice(i, i + size) for i in range(0, keys.shape[0], size)]
    scores = []
    for block in blocks:
        s = lax.dot_general(
            q, keys[block], (((1,), (1,)), ((), ())), preferred_element_type=jnp.float32
        )
        if live is not None:
            s = jnp.where(live[:, block], s, MASKED)
        scores.append(s)
    tops, sums = [], []
    for block, s in zip(blocks, scores):
        t = jnp.max(s, axis=1, keepdims=True)
        p = jnp.exp2((s - t) * SCALE2).astype(jnp.bfloat16)
        tops.append(t)
        sums.append(jnp.dot(p, values[block], preferred_element_type=jnp.float32))
    m = functools.reduce(jnp.maximum, tops)
    o = functools.reduce(
        jnp.add, [x * jnp.exp2((t - m) * SCALE2) for x, t in zip(sums, tops)]
    )
    return m, o


def kernel(
    n,
    kv,
    q_hbm,
    rk_hbm,
    rv_hbm,
    bk_hbm,
    bv_hbm,
    id_ref,
    len_ref,
    out_ref,
    qg,
    rk,
    rv,
    bk,
    bv,
    root_o,
    root_m,
    root_l,
    branch_o,
    part,
    part_l,
    recv,
    recv_l,
    own_sem,
    load_sem,
    qsend_sem,
    qrecv_sem,
    psend_sem,
    precv_sem,
    lsend_sem,
    lrecv_sem,
):
    me = lax.axis_index("seq")
    rows = q_hbm.shape[0]
    all_rows = n * rows
    chunks = kv * CUT
    heads = GROUP // CUT
    width = heads * HEAD_DIM
    branches = bk_hbm.shape[0]
    branch_len = bk_hbm.shape[1]
    most = 2 * rows // branches
    slots = branches * most
    has_left, has_right = me > 0, me < n - 1
    last = me == n - 1

    barrier = pltpu.get_barrier_semaphore()

    for k in range(1, REACH + 1):

        @pl.when(me >= k)
        def _():
            pl.semaphore_signal(barrier, inc=1, device_id={"seq": me - k}, device_id_type=MESH)

        @pl.when(me < n - k)
        def _():
            pl.semaphore_signal(barrier, inc=1, device_id={"seq": me + k}, device_id_type=MESH)

    def head_cols(f):
        return pl.ds(f * HEAD_DIM, HEAD_DIM)

    def shard_rows(s):
        return pl.ds(pl.multiple_of(s * rows, rows), rows)

    own = [
        pltpu.make_async_copy(
            q_hbm.at[:, pl.ds(c * width, width)], qg.at[c, shard_rows(me)], own_sem.at[c]
        )
        for c in range(chunks)
    ]
    loads, bloads = [], []
    for f in range(kv):
        loads += [
            pltpu.make_async_copy(rk_hbm.at[:, head_cols(f)], rk.at[f], load_sem.at[0, f, 0]),
            pltpu.make_async_copy(
                rv_hbm.at[:, head_cols(f)], rv.at[f, :, pl.ds(0, HEAD_DIM)], load_sem.at[1, f, 0]
            ),
        ]
        for b in range(branches):
            bloads += [
                pltpu.make_async_copy(
                    bk_hbm.at[b, :, head_cols(f)], bk.at[f, b], load_sem.at[2, f, b]
                ),
                pltpu.make_async_copy(
                    bv_hbm.at[b, :, head_cols(f)],
                    bv.at[f, b, :, pl.ds(0, HEAD_DIM)],
                    load_sem.at[3, f, b],
                ),
            ]

    def q_copy(c, s, d, slot):
        block = qg.at[c, shard_rows(s)]
        return pltpu.make_async_remote_copy(
            src_ref=block,
            dst_ref=block,
            send_sem=qsend_sem.at[c, slot],
            recv_sem=qrecv_sem.at[c, s],
            device_id={"seq": d},
            device_id_type=MESH,
        )

    def targets(do):
        for k in range(1, REACH + 1):

            @pl.when(me < n - k)
            def _():
                do(me + k, 2 * k - 2)

            @pl.when(me >= k)
            def _():
                do(me - k, 2 * k - 1)

    def send_own(c):
        targets(lambda d, slot: q_copy(c, me, d, slot).start())

    def passed(hop):
        return hop >= REACH

    def forward(t):
        for hop in range(1, n):
            c = t - hop + 1
            there = (c >= 0) & (c < chunks)
            left, right = me - hop, me + hop

            @pl.when(there & (left >= 0))
            def _():
                q_copy(c, left, me, 0).wait_recv()
                if passed(hop):

                    @pl.when(has_right)
                    def _():
                        q_copy(c, left, me + 1, 2 * hop).start()

            @pl.when(there & (right < n))
            def _():
                q_copy(c, right, me, 0).wait_recv()
                if passed(hop):

                    @pl.when(has_left)
                    def _():
                        q_copy(c, right, me - 1, 2 * hop + 1).start()

    def sent(c):
        targets(lambda d, slot: q_copy(c, me, d, slot).wait_send())
        for hop in range(REACH, n - 1):
            left, right = me - hop, me + hop

            @pl.when((left >= 0) & has_right)
            def _():
                q_copy(c, left, me + 1, 2 * hop).wait_send()

            @pl.when((right < n) & has_left)
            def _():
                q_copy(c, right, me - 1, 2 * hop + 1).wait_send()

    def greet():
        near = jnp.minimum(me, REACH) + jnp.minimum(n - 1 - me, REACH)
        pl.semaphore_wait(barrier, near)
        for c in range(chunks):
            send_own(c)

    for copy in own:
        copy.start()

    @pl.when(last)
    def _():
        for copy in own:
            copy.wait()
        greet()

    for copy in loads + bloads:
        copy.start()
    for f in range(kv):
        rv[f, :, HEAD_DIM:] = jnp.ones((rv.shape[1], HEAD_DIM), jnp.bfloat16)
        for b in range(branches):
            bv[f, b, :, HEAD_DIM:] = jnp.ones((branch_len, HEAD_DIM), jnp.bfloat16)

    slot = lax.broadcasted_iota(jnp.int32, (slots, all_rows), 0)
    named = id_ref[...] == me * branches + slot // most
    named_b = jnp.where(named, 1.0, 0.0).astype(jnp.bfloat16)
    tri = jnp.where(
        lax.broadcasted_iota(jnp.int32, (all_rows, all_rows), 0)
        <= lax.broadcasted_iota(jnp.int32, (all_rows, all_rows), 1),
        1.0,
        0.0,
    ).astype(jnp.bfloat16)
    rank = jnp.dot(named_b, tri, preferred_element_type=jnp.float32)
    pick_f = jnp.where(named & (rank == (lax.rem(slot, most) + 1).astype(jnp.float32)), 1.0, 0.0)
    pick_b = pick_f.astype(jnp.bfloat16)
    place_b = pick_f.T.astype(jnp.bfloat16)
    held = jnp.dot(
        place_b, jnp.ones((slots, HEAD_DIM), jnp.bfloat16), preferred_element_type=jnp.float32
    )

    lane = lax.broadcasted_iota(jnp.int32, (rows, HEAD_DIM), 1)
    slot_lane = lax.broadcasted_iota(jnp.int32, (slots, HEAD_DIM), 1)
    most_lane = lax.broadcasted_iota(jnp.int32, (most, HEAD_DIM), 1)
    position = lax.broadcasted_iota(jnp.int32, (1, branch_len), 1)

    def split(x, lanes):
        high = x.astype(jnp.bfloat16).astype(jnp.float32)
        rest = x - high
        mid = rest.astype(jnp.bfloat16).astype(jnp.float32)
        low = rest - mid
        return jnp.where(
            lanes < GROUP,
            high,
            jnp.where(
                lanes < 2 * GROUP, pltpu.roll(mid, GROUP, axis=1), pltpu.roll(low, 2 * GROUP, axis=1)
            ),
        ).astype(jnp.bfloat16)

    def whole(x):
        return (
            x
            + pltpu.roll(x, HEAD_DIM - GROUP, axis=1)
            + pltpu.roll(x, HEAD_DIM - 2 * GROUP, axis=1)
        )

    def p_copy(c, d, src):
        return pltpu.make_async_remote_copy(
            src_ref=part.at[c, d],
            dst_ref=recv.at[c, src],
            send_sem=psend_sem.at[c, d],
            recv_sem=precv_sem.at[c, src],
            device_id={"seq": d},
            device_id_type=MESH,
        )

    def l_copy(c, d, src):
        return pltpu.make_async_remote_copy(
            src_ref=part_l.at[c, d],
            dst_ref=recv_l.at[c, src],
            send_sem=lsend_sem.at[c, d],
            recv_sem=lrecv_sem.at[c, src],
            device_id={"seq": d},
            device_id_type=MESH,
        )

    def others(do):
        for d in range(n):

            @pl.when(me != d)
            def _(d=d):
                do(d)

    def root(f, pairs, count):
        q = jnp.concatenate(
            [
                qg[c, shard_rows(s), h * HEAD_DIM : (h + 1) * HEAD_DIM]
                for c, s in pairs
                for h in range(heads)
            ],
            axis=0,
        )
        m, o = attend(q, rk[f], rv[f])
        for i, (c, s) in enumerate(pairs):
            ms = jnp.zeros((rows, HEAD_DIM), jnp.float32)
            ls = jnp.ones((rows, HEAD_DIM), jnp.float32)
            for h in range(heads):
                at = (i * heads + h) * rows
                block = slice(at, at + rows)
                root_o[c, shard_rows(s), h * HEAD_DIM : (h + 1) * HEAD_DIM] = o[block, :HEAD_DIM]
                ms = jnp.where(lane == h, m[block], ms)
                ls = jnp.where(lane == h, o[block, HEAD_DIM:], ls)
            root_m[c, shard_rows(s)] = ms
            root_l[c, shard_rows(s)] = ls

    def root_own(f, carry):
        root(f, [(f * CUT + i, me) for i in range(CUT)], CUT)
        return carry

    def root_others(c):
        size = min(SHARDS, n - 1)
        groups = (n - 1) // size

        def one(g, carry):
            root(c // CUT, [(c, lax.rem(me + 1 + g * size + i, n)) for i in range(size)], size)
            return carry

        lax.fori_loop(0, groups, one, 0)
        rest = n - 1 - groups * size
        if rest:
            root(c // CUT, [(c, lax.rem(me + n - 1 - i, n)) for i in range(rest)], rest)

    def branch(c):
        f = c // CUT
        picked = jnp.dot(pick_b, qg[c], preferred_element_type=jnp.float32).astype(jnp.bfloat16)
        lses = []
        for b in range(branches):
            live = position < len_ref[me * branches + b]
            mine = picked[b * most : (b + 1) * most]
            q = jnp.concatenate(
                [mine[:, h * HEAD_DIM : (h + 1) * HEAD_DIM] for h in range(heads)], axis=0
            )
            m, o = attend(q, bk[f, b], bv[f, b], live)
            ms = jnp.zeros((most, HEAD_DIM), jnp.float32)
            ls = jnp.ones((most, HEAD_DIM), jnp.float32)
            for h in range(heads):
                block = slice(h * most, (h + 1) * most)
                branch_o[b * most : (b + 1) * most, h * HEAD_DIM : (h + 1) * HEAD_DIM] = (
                    o[block, :HEAD_DIM] / o[block, HEAD_DIM:]
                ).astype(jnp.bfloat16)
                ms = jnp.where(most_lane == h, m[block], ms)
                ls = jnp.where(most_lane == h, o[block, HEAD_DIM:], ls)
            lses.append(ms * SCALE2 + jnp.log2(ls))
        branch_o[:, width:] = split(jnp.concatenate(lses, axis=0), slot_lane)

    def mix(c):
        put = jnp.dot(place_b, branch_o[...], preferred_element_type=jnp.float32)
        put_s = jnp.where(held > 0.5, whole(put[:, width:]), MASKED)
        root_sum = root_l[c]
        root_lse = root_m[c] * SCALE2 + jnp.log2(root_sum)
        top = jnp.maximum(root_lse, put_s)
        root_w = jnp.exp2(root_lse - top)
        branch_w = jnp.exp2(put_s - top)
        total = root_w + branch_w
        joined = (top + jnp.log2(total)).T[:GROUP]
        root_c = root_w / (total * root_sum)
        branch_c = branch_w / total
        for d in range(n):
            at = d * rows
            tile, turn = at // HEAD_DIM * HEAD_DIM, at % HEAD_DIM
            x = joined[:, tile : tile + HEAD_DIM]
            part_l[c, d] = pltpu.roll(x, HEAD_DIM - turn, axis=1) if turn else x
        for h in range(heads):
            cols = slice(h * HEAD_DIM, (h + 1) * HEAD_DIM)
            mixed = (
                root_o[c, :, cols] * root_c[:, h : h + 1] + put[:, cols] * branch_c[:, h : h + 1]
            ).astype(jnp.bfloat16)
            for d in range(n):
                part[c, d, :, cols] = mixed[d * rows : (d + 1) * rows]

    def finish(c, carry):
        for k in range(1, n):
            s = lax.rem(me + k, n)
            l_copy(c, me, s).wait_recv()
            p_copy(c, me, s).wait_recv()
        recv[c, me] = part[c, me]
        recv_l[c, me] = part_l[c, me]
        lse = [recv_l[c, s] for s in range(n)]
        top = functools.reduce(jnp.maximum, lse)
        weights = [jnp.exp2(x - top) for x in lse]
        total = functools.reduce(jnp.add, weights)
        coefs = [w / total for w in weights]
        spare = HEAD_DIM - n * GROUP
        if spare > 0:
            coefs.append(jnp.zeros((spare, HEAD_DIM), jnp.float32))
        coef = jnp.concatenate(coefs, axis=0).T[:rows]
        for h in range(heads):
            cols = slice(h * HEAD_DIM, (h + 1) * HEAD_DIM)
            acc = recv[c, 0, :, cols].astype(jnp.float32) * coef[:, h : h + 1]
            for s in range(1, n):
                at = s * GROUP + h
                acc += recv[c, s, :, cols].astype(jnp.float32) * coef[:, at : at + 1]
            out_ref[c, :, cols] = acc.astype(jnp.bfloat16)
        return carry

    @pl.when(jnp.logical_not(last))
    def _():
        for copy in own:
            copy.wait()
        greet()

    for copy in loads:
        copy.wait()
    root_own(0, 0)

    if kv > 1:
        lax.fori_loop(1, kv, root_own, 0)
    lax.fori_loop(0, n - 1, lambda t, x: (forward(t), x)[1], 0)
    for copy in bloads:
        copy.wait()

    def step(c, carry):
        root_others(c)

        branch(c)
        mix(c)

        def go(d):
            l_copy(c, d, me).start()
            p_copy(c, d, me).start()

        others(go)
        forward(c + n - 1)
        return carry

    lax.fori_loop(0, chunks, step, 0)
    lax.fori_loop(0, chunks, finish, 0)

    def done(c, carry):
        sent(c)

        def gone(d):
            l_copy(c, d, me).wait_send()
            p_copy(c, d, me).wait_send()

        others(gone)
        return carry

    lax.fori_loop(0, chunks, done, 0)


def body(n, queries, root_keys, root_values, branch_keys, branch_values, branch_id, doc_len):
    rows = queries.shape[0]
    kv = root_keys.shape[1] // HEAD_DIM
    root_len = root_keys.shape[0]
    branches, branch_len = branch_keys.shape[:2]
    chunks = kv * CUT
    width = GROUP // CUT * HEAD_DIM
    all_rows = n * rows
    most = 2 * rows // branches
    slots = branches * most
    any_spec = pl.BlockSpec(memory_space=pl.ANY)
    bf16, f32 = jnp.bfloat16, jnp.float32
    dma = pltpu.SemaphoreType.DMA
    out = pl.pallas_call(
        functools.partial(kernel, n, kv),
        out_shape=jax.ShapeDtypeStruct((chunks, rows, width), bf16),
        in_specs=[any_spec] * 5
        + [pl.BlockSpec(memory_space=pltpu.VMEM), pl.BlockSpec(memory_space=pltpu.SMEM)],
        out_specs=pl.BlockSpec(memory_space=pltpu.VMEM),
        scratch_shapes=[
            pltpu.VMEM((chunks, all_rows, width), bf16),
            pltpu.VMEM((kv, root_len, HEAD_DIM), bf16),
            pltpu.VMEM((kv, root_len, 2 * HEAD_DIM), bf16),
            pltpu.VMEM((kv, branches, branch_len, HEAD_DIM), bf16),
            pltpu.VMEM((kv, branches, branch_len, 2 * HEAD_DIM), bf16),
            pltpu.VMEM((chunks, all_rows, width), f32),
            pltpu.VMEM((chunks, all_rows, HEAD_DIM), f32),
            pltpu.VMEM((chunks, all_rows, HEAD_DIM), f32),
            pltpu.VMEM((slots, width + HEAD_DIM), bf16),
            pltpu.VMEM((chunks, n, rows, width), bf16),
            pltpu.VMEM((chunks, n, GROUP, HEAD_DIM), f32),
            pltpu.VMEM((chunks, n, rows, width), bf16),
            pltpu.VMEM((chunks, n, GROUP, HEAD_DIM), f32),
            dma((chunks,)),
            dma((4, kv, branches)),
            dma((chunks, 2 * n)),
            dma((chunks, n)),
            dma((chunks, n)),
            dma((chunks, n)),
            dma((chunks, n)),
            dma((chunks, n)),
        ],
        compiler_params=pltpu.CompilerParams(
            collective_id=0, has_side_effects=True, vmem_limit_bytes=60 * 1024 * 1024
        ),
    )(queries, root_keys, root_values, branch_keys, branch_values, branch_id.reshape(1, -1), doc_len)
    return out.transpose(1, 0, 2).reshape(queries.shape)


def solution(mesh):
    in_specs = (
        P(("parts", "seq"), "head"),
        P(("parts", "seq"), "head"),
        P(("parts", "seq"), "head"),
        P(("parts", "seq"), None, "head"),
        P(("parts", "seq"), None, "head"),
        P("parts", None),
        P("parts"),
    )
    out_specs = P(("parts", "seq"), "head")
    return jax.shard_map(
        functools.partial(body, mesh.shape["seq"]),
        mesh=mesh,
        in_specs=in_specs,
        out_specs=out_specs,
        check_vma=False,
    )
```

```python
import functools

import jax
import jax.numpy as jnp
from jax import lax
from jax.experimental import pallas as pl
from jax.experimental.pallas import tpu as pltpu
from jax.sharding import PartitionSpec as P

QHEADS = 64
KVHEADS = 8
HEAD_DIM = 128
GROUP = QHEADS // KVHEADS
MESH = pl.DeviceIdType.MESH
LOG2E = 1.4426950408889634
SCALE2 = HEAD_DIM ** (-0.5) * LOG2E
MASKED = -1e30
KEY_BLOCK = 512
CUT = 1
REACH = 1


def attend(q, keys, values, live=None):
    size = min(KEY_BLOCK, keys.shape[0])
    blocks = [slice(i, i + size) for i in range(0, keys.shape[0], size)]
    scores = []
    for block in blocks:
        s = lax.dot_general(
            q, keys[block], (((1,), (1,)), ((), ())), preferred_element_type=jnp.float32
        )
        if live is not None:
            s = jnp.where(live[:, block], s, MASKED)
        scores.append(s)
    tops, sums = [], []
    for block, s in zip(blocks, scores):
        t = jnp.max(s, axis=1, keepdims=True)
        p = jnp.exp2((s - t) * SCALE2).astype(jnp.bfloat16)
        tops.append(t)
        sums.append(jnp.dot(p, values[block], preferred_element_type=jnp.float32))
    m = functools.reduce(jnp.maximum, tops)
    o = functools.reduce(
        jnp.add, [x * jnp.exp2((t - m) * SCALE2) for x, t in zip(sums, tops)]
    )
    return m, o


def kernel(
    n,
    kv,
    q_hbm,
    rk_hbm,
    rv_hbm,
    bk_hbm,
    bv_hbm,
    id_ref,
    len_ref,
    out_ref,
    qg,
    rk,
    rv,
    bk,
    bv,
    own_o,
    own_m,
    own_l,
    branch_o,
    put,
    part,
    part_l,
    recv,
    recv_l,
    own_sem,
    load_sem,
    qsend_sem,
    qrecv_sem,
    psend_sem,
    precv_sem,
    lsend_sem,
    lrecv_sem,
):
    me = lax.axis_index("seq")
    rows = q_hbm.shape[0]
    all_rows = n * rows
    chunks = kv * CUT
    heads = GROUP // CUT
    width = heads * HEAD_DIM
    branches = bk_hbm.shape[0]
    branch_len = bk_hbm.shape[1]
    most = 2 * rows // branches
    slots = branches * most
    has_left, has_right = me > 0, me < n - 1
    last = me == n - 1

    barrier = pltpu.get_barrier_semaphore()

    for k in range(1, REACH + 1):

        @pl.when(me >= k)
        def _():
            pl.semaphore_signal(barrier, inc=1, device_id={"seq": me - k}, device_id_type=MESH)

        @pl.when(me < n - k)
        def _():
            pl.semaphore_signal(barrier, inc=1, device_id={"seq": me + k}, device_id_type=MESH)

    def head_cols(f):
        return pl.ds(f * HEAD_DIM, HEAD_DIM)

    def shard_rows(s):
        return pl.ds(pl.multiple_of(s * rows, rows), rows)

    own = [
        pltpu.make_async_copy(
            q_hbm.at[:, pl.ds(c * width, width)], qg.at[c, shard_rows(me)], own_sem.at[c]
        )
        for c in range(chunks)
    ]
    loads, bloads = [], []
    for f in range(kv):
        loads += [
            pltpu.make_async_copy(rk_hbm.at[:, head_cols(f)], rk.at[f], load_sem.at[0, f, 0]),
            pltpu.make_async_copy(
                rv_hbm.at[:, head_cols(f)], rv.at[f, :, pl.ds(0, HEAD_DIM)], load_sem.at[1, f, 0]
            ),
        ]
        for b in range(branches):
            bloads += [
                pltpu.make_async_copy(
                    bk_hbm.at[b, :, head_cols(f)], bk.at[f, b], load_sem.at[2, f, b]
                ),
                pltpu.make_async_copy(
                    bv_hbm.at[b, :, head_cols(f)],
                    bv.at[f, b, :, pl.ds(0, HEAD_DIM)],
                    load_sem.at[3, f, b],
                ),
            ]

    def q_copy(c, s, d, slot):
        block = qg.at[c, shard_rows(s)]
        return pltpu.make_async_remote_copy(
            src_ref=block,
            dst_ref=block,
            send_sem=qsend_sem.at[c, slot],
            recv_sem=qrecv_sem.at[c, s],
            device_id={"seq": d},
            device_id_type=MESH,
        )

    def targets(do):
        for k in range(1, REACH + 1):

            @pl.when(me < n - k)
            def _():
                do(me + k, 2 * k - 2)

            @pl.when(me >= k)
            def _():
                do(me - k, 2 * k - 1)

    def send_own(c):
        targets(lambda d, slot: q_copy(c, me, d, slot).start())

    def passed(hop):
        return hop >= REACH

    def forward(t):
        for hop in range(1, n):
            c = t - hop + 1
            there = (c >= 0) & (c < chunks)
            left, right = me - hop, me + hop

            @pl.when(there & (left >= 0))
            def _():
                q_copy(c, left, me, 0).wait_recv()
                if passed(hop):

                    @pl.when(has_right)
                    def _():
                        q_copy(c, left, me + 1, 2 * hop).start()

            @pl.when(there & (right < n))
            def _():
                q_copy(c, right, me, 0).wait_recv()
                if passed(hop):

                    @pl.when(has_left)
                    def _():
                        q_copy(c, right, me - 1, 2 * hop + 1).start()

    def sent(c):
        targets(lambda d, slot: q_copy(c, me, d, slot).wait_send())
        for hop in range(REACH, n - 1):
            left, right = me - hop, me + hop

            @pl.when((left >= 0) & has_right)
            def _():
                q_copy(c, left, me + 1, 2 * hop).wait_send()

            @pl.when((right < n) & has_left)
            def _():
                q_copy(c, right, me - 1, 2 * hop + 1).wait_send()

    def greet():
        near = jnp.minimum(me, REACH) + jnp.minimum(n - 1 - me, REACH)
        pl.semaphore_wait(barrier, near)
        for c in range(chunks):
            send_own(c)

    for copy in own:
        copy.start()

    @pl.when(last)
    def _():
        for copy in own:
            copy.wait()
        greet()

    for copy in loads + bloads:
        copy.start()
    for f in range(kv):
        rv[f, :, HEAD_DIM:] = jnp.ones((rv.shape[1], HEAD_DIM), jnp.bfloat16)
        for b in range(branches):
            bv[f, b, :, HEAD_DIM:] = jnp.ones((branch_len, HEAD_DIM), jnp.bfloat16)

    slot = lax.broadcasted_iota(jnp.int32, (slots, all_rows), 0)
    named = id_ref[...] == me * branches + slot // most
    named_b = jnp.where(named, 1.0, 0.0).astype(jnp.bfloat16)
    tri = jnp.where(
        lax.broadcasted_iota(jnp.int32, (all_rows, all_rows), 0)
        <= lax.broadcasted_iota(jnp.int32, (all_rows, all_rows), 1),
        1.0,
        0.0,
    ).astype(jnp.bfloat16)
    rank = jnp.dot(named_b, tri, preferred_element_type=jnp.float32)
    pick_f = jnp.where(named & (rank == (lax.rem(slot, most) + 1).astype(jnp.float32)), 1.0, 0.0)
    pick_b = pick_f.astype(jnp.bfloat16)
    place_b = pick_f.T.astype(jnp.bfloat16)
    held = jnp.dot(
        place_b, jnp.ones((slots, HEAD_DIM), jnp.bfloat16), preferred_element_type=jnp.float32
    )

    lane = lax.broadcasted_iota(jnp.int32, (rows, HEAD_DIM), 1)
    slot_lane = lax.broadcasted_iota(jnp.int32, (slots, HEAD_DIM), 1)
    most_lane = lax.broadcasted_iota(jnp.int32, (most, HEAD_DIM), 1)
    position = lax.broadcasted_iota(jnp.int32, (1, branch_len), 1)

    def split(x, lanes):
        high = x.astype(jnp.bfloat16).astype(jnp.float32)
        rest = x - high
        mid = rest.astype(jnp.bfloat16).astype(jnp.float32)
        low = rest - mid
        return jnp.where(
            lanes < GROUP,
            high,
            jnp.where(
                lanes < 2 * GROUP, pltpu.roll(mid, GROUP, axis=1), pltpu.roll(low, 2 * GROUP, axis=1)
            ),
        ).astype(jnp.bfloat16)

    def whole(x):
        return (
            x
            + pltpu.roll(x, HEAD_DIM - GROUP, axis=1)
            + pltpu.roll(x, HEAD_DIM - 2 * GROUP, axis=1)
        )

    def p_copy(c, d, src):
        return pltpu.make_async_remote_copy(
            src_ref=part.at[c, d],
            dst_ref=recv.at[c, src],
            send_sem=psend_sem.at[c, d],
            recv_sem=precv_sem.at[c, src],
            device_id={"seq": d},
            device_id_type=MESH,
        )

    def l_copy(c, d, src):
        return pltpu.make_async_remote_copy(
            src_ref=part_l.at[c, d],
            dst_ref=recv_l.at[c, src],
            send_sem=lsend_sem.at[c, d],
            recv_sem=lrecv_sem.at[c, src],
            device_id={"seq": d},
            device_id_type=MESH,
        )

    def others(do):
        for d in range(n):

            @pl.when(me != d)
            def _(d=d):
                do(d)

    def root(f, s):
        q = jnp.concatenate(
            [qg[f, shard_rows(s), h * HEAD_DIM : (h + 1) * HEAD_DIM] for h in range(heads)],
            axis=0,
        )
        m, o = attend(q, rk[f], rv[f])
        ms = jnp.zeros((rows, HEAD_DIM), jnp.float32)
        ls = jnp.ones((rows, HEAD_DIM), jnp.float32)
        for h in range(heads):
            block = slice(h * rows, (h + 1) * rows)
            ms = jnp.where(lane == h, m[block], ms)
            ls = jnp.where(lane == h, o[block, HEAD_DIM:], ls)
        return o[:, :HEAD_DIM], ms, ls

    def root_own(f, carry):
        own_o[f], own_m[f], own_l[f] = root(f, me)
        return carry

    def branch(c):
        f = c // CUT
        picked = jnp.dot(pick_b, qg[c], preferred_element_type=jnp.float32).astype(jnp.bfloat16)
        lses = []
        for b in range(branches):
            live = position < len_ref[me * branches + b]
            mine = picked[b * most : (b + 1) * most]
            q = jnp.concatenate(
                [mine[:, h * HEAD_DIM : (h + 1) * HEAD_DIM] for h in range(heads)], axis=0
            )
            m, o = attend(q, bk[f, b], bv[f, b], live)
            ms = jnp.zeros((most, HEAD_DIM), jnp.float32)
            ls = jnp.ones((most, HEAD_DIM), jnp.float32)
            for h in range(heads):
                block = slice(h * most, (h + 1) * most)
                branch_o[b * most : (b + 1) * most, h * HEAD_DIM : (h + 1) * HEAD_DIM] = (
                    o[block, :HEAD_DIM] / o[block, HEAD_DIM:]
                ).astype(jnp.bfloat16)
                ms = jnp.where(most_lane == h, m[block], ms)
                ls = jnp.where(most_lane == h, o[block, HEAD_DIM:], ls)
            lses.append(ms * SCALE2 + jnp.log2(ls))
        branch_o[:, width:] = split(jnp.concatenate(lses, axis=0), slot_lane)
        moved = jnp.dot(place_b, branch_o[...], preferred_element_type=jnp.float32)
        put[:, :width] = moved[:, :width]
        put[:, width:] = jnp.where(held > 0.5, whole(moved[:, width:]), MASKED)

    def mix(f, d, o, ms, root_sum):
        put_s = put[shard_rows(d), width:]
        root_lse = ms * SCALE2 + jnp.log2(root_sum)
        top = jnp.maximum(root_lse, put_s)
        root_w = jnp.exp2(root_lse - top)
        branch_w = jnp.exp2(put_s - top)
        total = root_w + branch_w
        root_c = root_w / (total * root_sum)
        branch_c = branch_w / total
        part_l[f, d, :, :rows] = (top + jnp.log2(total)).T[:GROUP]
        for h in range(heads):
            cols = slice(h * HEAD_DIM, (h + 1) * HEAD_DIM)
            part[f, d, :, cols] = (
                o[h * rows : (h + 1) * rows] * root_c[:, h : h + 1]
                + put[shard_rows(d), cols] * branch_c[:, h : h + 1]
            ).astype(jnp.bfloat16)

    def finish(c, carry):
        for k in range(1, n):
            s = lax.rem(me + k, n)
            l_copy(c, me, s).wait_recv()
            p_copy(c, me, s).wait_recv()
        recv[c, me] = part[c, me]
        recv_l[c, me] = part_l[c, me]
        lse = [recv_l[c, s] for s in range(n)]
        top = functools.reduce(jnp.maximum, lse)
        weights = [jnp.exp2(x - top) for x in lse]
        total = functools.reduce(jnp.add, weights)
        coefs = [w / total for w in weights]
        spare = HEAD_DIM - n * GROUP
        if spare > 0:
            coefs.append(jnp.zeros((spare, HEAD_DIM), jnp.float32))
        coef = jnp.concatenate(coefs, axis=0).T[:rows]
        for h in range(heads):
            cols = slice(h * HEAD_DIM, (h + 1) * HEAD_DIM)
            acc = recv[c, 0, :, cols].astype(jnp.float32) * coef[:, h : h + 1]
            for s in range(1, n):
                at = s * GROUP + h
                acc += recv[c, s, :, cols].astype(jnp.float32) * coef[:, at : at + 1]
            out_ref[c, :, cols] = acc.astype(jnp.bfloat16)
        return carry

    @pl.when(jnp.logical_not(last))
    def _():
        for copy in own:
            copy.wait()
        greet()

    for copy in loads:
        copy.wait()
    root_own(0, 0)

    if kv > 1:
        lax.fori_loop(1, kv, root_own, 0)
    lax.fori_loop(0, n - 1, lambda t, x: (forward(t), x)[1], 0)
    for copy in bloads:
        copy.wait()

    def step(f, carry):
        branch(f)

        def give(i, carry):
            d = jnp.where(i < me, i, i + 1)
            o, ms, ls = root(f, d)
            mix(f, d, o, ms, ls)
            l_copy(f, d, me).start()
            p_copy(f, d, me).start()
            return carry

        lax.fori_loop(0, n - 1, give, 0)
        forward(f + n - 1)
        mix(f, me, own_o[f], own_m[f], own_l[f])
        return carry

    lax.fori_loop(0, chunks, step, 0)
    lax.fori_loop(0, chunks, finish, 0)

    def done(c, carry):
        sent(c)

        def gone(d):
            l_copy(c, d, me).wait_send()
            p_copy(c, d, me).wait_send()

        others(gone)
        return carry

    lax.fori_loop(0, chunks, done, 0)


def body(n, queries, root_keys, root_values, branch_keys, branch_values, branch_id, doc_len):
    rows = queries.shape[0]
    kv = root_keys.shape[1] // HEAD_DIM
    root_len = root_keys.shape[0]
    branches, branch_len = branch_keys.shape[:2]
    chunks = kv * CUT
    width = GROUP // CUT * HEAD_DIM
    all_rows = n * rows
    most = 2 * rows // branches
    slots = branches * most
    any_spec = pl.BlockSpec(memory_space=pl.ANY)
    bf16, f32 = jnp.bfloat16, jnp.float32
    dma = pltpu.SemaphoreType.DMA
    out = pl.pallas_call(
        functools.partial(kernel, n, kv),
        out_shape=jax.ShapeDtypeStruct((chunks, rows, width), bf16),
        in_specs=[any_spec] * 5
        + [pl.BlockSpec(memory_space=pltpu.VMEM), pl.BlockSpec(memory_space=pltpu.SMEM)],
        out_specs=pl.BlockSpec(memory_space=pltpu.VMEM),
        scratch_shapes=[
            pltpu.VMEM((chunks, all_rows, width), bf16),
            pltpu.VMEM((kv, root_len, HEAD_DIM), bf16),
            pltpu.VMEM((kv, root_len, 2 * HEAD_DIM), bf16),
            pltpu.VMEM((kv, branches, branch_len, HEAD_DIM), bf16),
            pltpu.VMEM((kv, branches, branch_len, 2 * HEAD_DIM), bf16),
            pltpu.VMEM((kv, GROUP * rows, HEAD_DIM), f32),
            pltpu.VMEM((kv, rows, HEAD_DIM), f32),
            pltpu.VMEM((kv, rows, HEAD_DIM), f32),
            pltpu.VMEM((slots, width + HEAD_DIM), bf16),
            pltpu.VMEM((all_rows, width + HEAD_DIM), f32),
            pltpu.VMEM((chunks, n, rows, width), bf16),
            pltpu.VMEM((chunks, n, GROUP, HEAD_DIM), f32),
            pltpu.VMEM((chunks, n, rows, width), bf16),
            pltpu.VMEM((chunks, n, GROUP, HEAD_DIM), f32),
            dma((chunks,)),
            dma((4, kv, branches)),
            dma((chunks, 2 * n)),
            dma((chunks, n)),
            dma((chunks, n)),
            dma((chunks, n)),
            dma((chunks, n)),
            dma((chunks, n)),
        ],
        compiler_params=pltpu.CompilerParams(
            collective_id=0, has_side_effects=True, vmem_limit_bytes=60 * 1024 * 1024
        ),
    )(queries, root_keys, root_values, branch_keys, branch_values, branch_id.reshape(1, -1), doc_len)
    return out.transpose(1, 0, 2).reshape(queries.shape)


def solution(mesh):
    in_specs = (
        P(("parts", "seq"), "head"),
        P(("parts", "seq"), "head"),
        P(("parts", "seq"), "head"),
        P(("parts", "seq"), None, "head"),
        P(("parts", "seq"), None, "head"),
        P("parts", None),
        P("parts"),
    )
    out_specs = P(("parts", "seq"), "head")
    return jax.shard_map(
        functools.partial(body, mesh.shape["seq"]),
        mesh=mesh,
        in_specs=in_specs,
        out_specs=out_specs,
        check_vma=False,
    )
```

```python
import functools

import jax
import jax.numpy as jnp
from jax import lax
from jax.experimental import pallas as pl
from jax.experimental.pallas import tpu as pltpu
from jax.sharding import PartitionSpec as P

QHEADS = 64
KVHEADS = 8
HEAD_DIM = 128
GROUP = QHEADS // KVHEADS
MESH = pl.DeviceIdType.MESH
LOG2E = 1.4426950408889634
SCALE2 = HEAD_DIM ** (-0.5) * LOG2E
MASKED = -1e30
KEY_BLOCK = 512
CUT = 1
REACH = 1


def attend(q, keys, values, live=None):
    size = min(KEY_BLOCK, keys.shape[0])
    blocks = [slice(i, i + size) for i in range(0, keys.shape[0], size)]
    scores = []
    for block in blocks:
        s = lax.dot_general(
            q, keys[block], (((1,), (1,)), ((), ())), preferred_element_type=jnp.float32
        )
        if live is not None:
            s = jnp.where(live[:, block], s, MASKED)
        scores.append(s)
    tops, sums = [], []
    for block, s in zip(blocks, scores):
        t = jnp.max(s, axis=1, keepdims=True)
        p = jnp.exp2((s - t) * SCALE2).astype(jnp.bfloat16)
        tops.append(t)
        sums.append(jnp.dot(p, values[block], preferred_element_type=jnp.float32))
    m = functools.reduce(jnp.maximum, tops)
    o = functools.reduce(
        jnp.add, [x * jnp.exp2((t - m) * SCALE2) for x, t in zip(sums, tops)]
    )
    return m, o


def kernel(
    n,
    kv,
    q_hbm,
    rk_hbm,
    rv_hbm,
    bk_hbm,
    bv_hbm,
    id_ref,
    len_ref,
    out_ref,
    qg,
    rk,
    rv,
    bk,
    bv,
    own_o,
    own_m,
    own_l,
    branch_o,
    put,
    part,
    part_l,
    recv,
    recv_l,
    done_o,
    own_sem,
    load_sem,
    qsend_sem,
    qrecv_sem,
    psend_sem,
    precv_sem,
    lsend_sem,
    lrecv_sem,
):
    me = lax.axis_index("seq")
    rows = q_hbm.shape[0]
    all_rows = n * rows
    chunks = kv * CUT
    heads = GROUP // CUT
    width = heads * HEAD_DIM
    branches = bk_hbm.shape[0]
    branch_len = bk_hbm.shape[1]
    most = 2 * rows // branches
    slots = branches * most
    has_left, has_right = me > 0, me < n - 1
    last = me == n - 1

    barrier = pltpu.get_barrier_semaphore()

    for k in range(1, REACH + 1):

        @pl.when(me >= k)
        def _():
            pl.semaphore_signal(barrier, inc=1, device_id={"seq": me - k}, device_id_type=MESH)

        @pl.when(me < n - k)
        def _():
            pl.semaphore_signal(barrier, inc=1, device_id={"seq": me + k}, device_id_type=MESH)

    def head_cols(f):
        return pl.ds(f * HEAD_DIM, HEAD_DIM)

    def shard_rows(s):
        return pl.ds(pl.multiple_of(s * rows, rows), rows)

    own = [
        pltpu.make_async_copy(
            q_hbm.at[:, pl.ds(c * width, width)], qg.at[c, shard_rows(me)], own_sem.at[c]
        )
        for c in range(chunks)
    ]
    loads, bloads = [], []
    for f in range(kv):
        loads += [
            pltpu.make_async_copy(rk_hbm.at[:, head_cols(f)], rk.at[f], load_sem.at[0, f, 0]),
            pltpu.make_async_copy(
                rv_hbm.at[:, head_cols(f)], rv.at[f, :, pl.ds(0, HEAD_DIM)], load_sem.at[1, f, 0]
            ),
        ]
        for b in range(branches):
            bloads += [
                pltpu.make_async_copy(
                    bk_hbm.at[b, :, head_cols(f)], bk.at[f, b], load_sem.at[2, f, b]
                ),
                pltpu.make_async_copy(
                    bv_hbm.at[b, :, head_cols(f)],
                    bv.at[f, b, :, pl.ds(0, HEAD_DIM)],
                    load_sem.at[3, f, b],
                ),
            ]

    def q_copy(c, s, d, slot):
        block = qg.at[c, shard_rows(s)]
        return pltpu.make_async_remote_copy(
            src_ref=block,
            dst_ref=block,
            send_sem=qsend_sem.at[c, slot],
            recv_sem=qrecv_sem.at[c, s],
            device_id={"seq": d},
            device_id_type=MESH,
        )

    def targets(do):
        for k in range(1, REACH + 1):

            @pl.when(me < n - k)
            def _():
                do(me + k, 2 * k - 2)

            @pl.when(me >= k)
            def _():
                do(me - k, 2 * k - 1)

    def send_own(c):
        targets(lambda d, slot: q_copy(c, me, d, slot).start())

    def passed(hop):
        return hop >= REACH

    def forward(t):
        for hop in range(1, n):
            c = t - hop + 1
            there = (c >= 0) & (c < chunks)
            left, right = me - hop, me + hop

            @pl.when(there & (left >= 0))
            def _():
                q_copy(c, left, me, 0).wait_recv()
                if passed(hop):

                    @pl.when(has_right)
                    def _():
                        q_copy(c, left, me + 1, 2 * hop).start()

            @pl.when(there & (right < n))
            def _():
                q_copy(c, right, me, 0).wait_recv()
                if passed(hop):

                    @pl.when(has_left)
                    def _():
                        q_copy(c, right, me - 1, 2 * hop + 1).start()

    def sent(c):
        targets(lambda d, slot: q_copy(c, me, d, slot).wait_send())
        for hop in range(REACH, n - 1):
            left, right = me - hop, me + hop

            @pl.when((left >= 0) & has_right)
            def _():
                q_copy(c, left, me + 1, 2 * hop).wait_send()

            @pl.when((right < n) & has_left)
            def _():
                q_copy(c, right, me - 1, 2 * hop + 1).wait_send()

    def greet():
        near = jnp.minimum(me, REACH) + jnp.minimum(n - 1 - me, REACH)
        pl.semaphore_wait(barrier, near)
        for c in range(chunks):
            send_own(c)

    for copy in own:
        copy.start()

    @pl.when(last)
    def _():
        for copy in own:
            copy.wait()
        greet()

    for copy in loads + bloads:
        copy.start()
    for f in range(kv):
        rv[f, :, HEAD_DIM:] = jnp.ones((rv.shape[1], HEAD_DIM), jnp.bfloat16)
        for b in range(branches):
            bv[f, b, :, HEAD_DIM:] = jnp.ones((branch_len, HEAD_DIM), jnp.bfloat16)

    slot = lax.broadcasted_iota(jnp.int32, (slots, all_rows), 0)
    named = id_ref[...] == me * branches + slot // most
    named_b = jnp.where(named, 1.0, 0.0).astype(jnp.bfloat16)
    tri = jnp.where(
        lax.broadcasted_iota(jnp.int32, (all_rows, all_rows), 0)
        <= lax.broadcasted_iota(jnp.int32, (all_rows, all_rows), 1),
        1.0,
        0.0,
    ).astype(jnp.bfloat16)
    rank = jnp.dot(named_b, tri, preferred_element_type=jnp.float32)
    pick_f = jnp.where(named & (rank == (lax.rem(slot, most) + 1).astype(jnp.float32)), 1.0, 0.0)
    pick_b = pick_f.astype(jnp.bfloat16)
    place_b = pick_f.T.astype(jnp.bfloat16)
    held = jnp.dot(
        place_b, jnp.ones((slots, HEAD_DIM), jnp.bfloat16), preferred_element_type=jnp.float32
    )

    lane = lax.broadcasted_iota(jnp.int32, (rows, HEAD_DIM), 1)
    slot_lane = lax.broadcasted_iota(jnp.int32, (slots, HEAD_DIM), 1)
    most_lane = lax.broadcasted_iota(jnp.int32, (most, HEAD_DIM), 1)
    position = lax.broadcasted_iota(jnp.int32, (1, branch_len), 1)

    def split(x, lanes):
        high = x.astype(jnp.bfloat16).astype(jnp.float32)
        rest = x - high
        mid = rest.astype(jnp.bfloat16).astype(jnp.float32)
        low = rest - mid
        return jnp.where(
            lanes < GROUP,
            high,
            jnp.where(
                lanes < 2 * GROUP, pltpu.roll(mid, GROUP, axis=1), pltpu.roll(low, 2 * GROUP, axis=1)
            ),
        ).astype(jnp.bfloat16)

    def whole(x):
        return (
            x
            + pltpu.roll(x, HEAD_DIM - GROUP, axis=1)
            + pltpu.roll(x, HEAD_DIM - 2 * GROUP, axis=1)
        )

    def p_copy(c, d, src):
        return pltpu.make_async_remote_copy(
            src_ref=part.at[c, d],
            dst_ref=recv.at[c, src],
            send_sem=psend_sem.at[c, d],
            recv_sem=precv_sem.at[c, src],
            device_id={"seq": d},
            device_id_type=MESH,
        )

    def l_copy(c, d, src):
        return pltpu.make_async_remote_copy(
            src_ref=part_l.at[c, d],
            dst_ref=recv_l.at[c, src],
            send_sem=lsend_sem.at[c, d],
            recv_sem=lrecv_sem.at[c, src],
            device_id={"seq": d},
            device_id_type=MESH,
        )

    def others(do):
        for d in range(n):

            @pl.when(me != d)
            def _(d=d):
                do(d)

    def root(f, s):
        q = jnp.concatenate(
            [qg[f, shard_rows(s), h * HEAD_DIM : (h + 1) * HEAD_DIM] for h in range(heads)],
            axis=0,
        )
        m, o = attend(q, rk[f], rv[f])
        ms = jnp.zeros((rows, HEAD_DIM), jnp.float32)
        ls = jnp.ones((rows, HEAD_DIM), jnp.float32)
        for h in range(heads):
            block = slice(h * rows, (h + 1) * rows)
            ms = jnp.where(lane == h, m[block], ms)
            ls = jnp.where(lane == h, o[block, HEAD_DIM:], ls)
        return o[:, :HEAD_DIM], ms, ls

    def root_own(f, carry):
        own_o[f], own_m[f], own_l[f] = root(f, me)
        return carry

    def branch(c):
        f = c // CUT
        picked = jnp.dot(pick_b, qg[c], preferred_element_type=jnp.float32).astype(jnp.bfloat16)
        lses = []
        for b in range(branches):
            live = position < len_ref[me * branches + b]
            mine = picked[b * most : (b + 1) * most]
            q = jnp.concatenate(
                [mine[:, h * HEAD_DIM : (h + 1) * HEAD_DIM] for h in range(heads)], axis=0
            )
            m, o = attend(q, bk[f, b], bv[f, b], live)
            ms = jnp.zeros((most, HEAD_DIM), jnp.float32)
            ls = jnp.ones((most, HEAD_DIM), jnp.float32)
            for h in range(heads):
                block = slice(h * most, (h + 1) * most)
                branch_o[b * most : (b + 1) * most, h * HEAD_DIM : (h + 1) * HEAD_DIM] = (
                    o[block, :HEAD_DIM] / o[block, HEAD_DIM:]
                ).astype(jnp.bfloat16)
                ms = jnp.where(most_lane == h, m[block], ms)
                ls = jnp.where(most_lane == h, o[block, HEAD_DIM:], ls)
            lses.append(ms * SCALE2 + jnp.log2(ls))
        branch_o[:, width:] = split(jnp.concatenate(lses, axis=0), slot_lane)
        moved = jnp.dot(place_b, branch_o[...], preferred_element_type=jnp.float32)
        put[:, :width] = moved[:, :width]
        put[:, width:] = jnp.where(held > 0.5, whole(moved[:, width:]), MASKED)

    def mix(f, d, o, ms, root_sum):
        put_s = put[shard_rows(d), width:]
        root_lse = ms * SCALE2 + jnp.log2(root_sum)
        top = jnp.maximum(root_lse, put_s)
        root_w = jnp.exp2(root_lse - top)
        branch_w = jnp.exp2(put_s - top)
        total = root_w + branch_w
        root_c = root_w / (total * root_sum)
        branch_c = branch_w / total
        part_l[f, d, :, :rows] = (top + jnp.log2(total)).T[:GROUP]
        for h in range(heads):
            cols = slice(h * HEAD_DIM, (h + 1) * HEAD_DIM)
            part[f, d, :, cols] = (
                o[h * rows : (h + 1) * rows] * root_c[:, h : h + 1]
                + put[shard_rows(d), cols] * branch_c[:, h : h + 1]
            ).astype(jnp.bfloat16)

    def finish(c, carry):
        for k in range(1, n):
            s = lax.rem(me + k, n)
            l_copy(c, me, s).wait_recv()
            p_copy(c, me, s).wait_recv()
        recv[c, me] = part[c, me]
        recv_l[c, me] = part_l[c, me]
        lse = [recv_l[c, s] for s in range(n)]
        top = functools.reduce(jnp.maximum, lse)
        weights = [jnp.exp2(x - top) for x in lse]
        total = functools.reduce(jnp.add, weights)
        coefs = [w / total for w in weights]
        spare = HEAD_DIM - n * GROUP
        if spare > 0:
            coefs.append(jnp.zeros((spare, HEAD_DIM), jnp.float32))
        coef = jnp.concatenate(coefs, axis=0).T[:rows]
        for h in range(heads):
            cols = slice(h * HEAD_DIM, (h + 1) * HEAD_DIM)
            acc = recv[c, 0, :, cols].astype(jnp.float32) * coef[:, h : h + 1]
            for s in range(1, n):
                at = s * GROUP + h
                acc += recv[c, s, :, cols].astype(jnp.float32) * coef[:, at : at + 1]
            done_o[c, :, cols] = acc.astype(jnp.bfloat16)
        pltpu.make_async_copy(done_o.at[c], out_ref.at[c], own_sem.at[c]).start()
        return carry

    @pl.when(jnp.logical_not(last))
    def _():
        for copy in own:
            copy.wait()
        greet()

    for copy in loads:
        copy.wait()
    root_own(0, 0)

    if kv > 1:
        lax.fori_loop(1, kv, root_own, 0)
    lax.fori_loop(0, n - 1, lambda t, x: (forward(t), x)[1], 0)
    for copy in bloads:
        copy.wait()

    def step(f, carry):
        branch(f)

        def give(i, carry):
            d = jnp.where(i < me, i, i + 1)
            o, ms, ls = root(f, d)
            mix(f, d, o, ms, ls)
            l_copy(f, d, me).start()
            p_copy(f, d, me).start()
            return carry

        lax.fori_loop(0, n - 1, give, 0)
        forward(f + n - 1)
        mix(f, me, own_o[f], own_m[f], own_l[f])
        return carry

    lax.fori_loop(0, chunks, step, 0)
    lax.fori_loop(0, chunks, finish, 0)

    def done(c, carry):
        sent(c)

        def gone(d):
            l_copy(c, d, me).wait_send()
            p_copy(c, d, me).wait_send()

        others(gone)
        return carry

    lax.fori_loop(0, chunks, done, 0)
    for c in range(chunks):
        pltpu.make_async_copy(done_o.at[c], out_ref.at[c], own_sem.at[c]).wait()


def body(n, queries, root_keys, root_values, branch_keys, branch_values, branch_id, doc_len):
    rows = queries.shape[0]
    kv = root_keys.shape[1] // HEAD_DIM
    root_len = root_keys.shape[0]
    branches, branch_len = branch_keys.shape[:2]
    chunks = kv * CUT
    width = GROUP // CUT * HEAD_DIM
    all_rows = n * rows
    most = 2 * rows // branches
    slots = branches * most
    any_spec = pl.BlockSpec(memory_space=pl.ANY)
    bf16, f32 = jnp.bfloat16, jnp.float32
    dma = pltpu.SemaphoreType.DMA
    out = pl.pallas_call(
        functools.partial(kernel, n, kv),
        out_shape=jax.ShapeDtypeStruct((chunks, rows, width), bf16),
        in_specs=[any_spec] * 5
        + [pl.BlockSpec(memory_space=pltpu.VMEM), pl.BlockSpec(memory_space=pltpu.SMEM)],
        out_specs=any_spec,
        scratch_shapes=[
            pltpu.VMEM((chunks, all_rows, width), bf16),
            pltpu.VMEM((kv, root_len, HEAD_DIM), bf16),
            pltpu.VMEM((kv, root_len, 2 * HEAD_DIM), bf16),
            pltpu.VMEM((kv, branches, branch_len, HEAD_DIM), bf16),
            pltpu.VMEM((kv, branches, branch_len, 2 * HEAD_DIM), bf16),
            pltpu.VMEM((kv, GROUP * rows, HEAD_DIM), f32),
            pltpu.VMEM((kv, rows, HEAD_DIM), f32),
            pltpu.VMEM((kv, rows, HEAD_DIM), f32),
            pltpu.VMEM((slots, width + HEAD_DIM), bf16),
            pltpu.VMEM((all_rows, width + HEAD_DIM), f32),
            pltpu.VMEM((chunks, n, rows, width), bf16),
            pltpu.VMEM((chunks, n, GROUP, HEAD_DIM), f32),
            pltpu.VMEM((chunks, n, rows, width), bf16),
            pltpu.VMEM((chunks, n, GROUP, HEAD_DIM), f32),
            pltpu.VMEM((chunks, rows, width), bf16),
            dma((chunks,)),
            dma((4, kv, branches)),
            dma((chunks, 2 * n)),
            dma((chunks, n)),
            dma((chunks, n)),
            dma((chunks, n)),
            dma((chunks, n)),
            dma((chunks, n)),
        ],
        compiler_params=pltpu.CompilerParams(
            collective_id=0, has_side_effects=True, vmem_limit_bytes=60 * 1024 * 1024
        ),
    )(queries, root_keys, root_values, branch_keys, branch_values, branch_id.reshape(1, -1), doc_len)
    return out.transpose(1, 0, 2).reshape(queries.shape)


def solution(mesh):
    in_specs = (
        P(("parts", "seq"), "head"),
        P(("parts", "seq"), "head"),
        P(("parts", "seq"), "head"),
        P(("parts", "seq"), None, "head"),
        P(("parts", "seq"), None, "head"),
        P("parts", None),
        P("parts"),
    )
    out_specs = P(("parts", "seq"), "head")
    return jax.shard_map(
        functools.partial(body, mesh.shape["seq"]),
        mesh=mesh,
        in_specs=in_specs,
        out_specs=out_specs,
        check_vma=False,
    )
```

```python
import functools

import jax
import jax.numpy as jnp
from jax import lax
from jax.experimental import pallas as pl
from jax.experimental.pallas import tpu as pltpu
from jax.sharding import PartitionSpec as P

QHEADS = 64
KVHEADS = 8
HEAD_DIM = 128
GROUP = QHEADS // KVHEADS
MESH = pl.DeviceIdType.MESH
LOG2E = 1.4426950408889634
SCALE2 = HEAD_DIM ** (-0.5) * LOG2E
MASKED = -1e30
KEY_BLOCK = 512
CUT = 1
REACH = 1


def attend(q, keys, values, live=None):
    size = min(KEY_BLOCK, keys.shape[0])
    blocks = [slice(i, i + size) for i in range(0, keys.shape[0], size)]
    scores = []
    for block in blocks:
        s = lax.dot_general(
            q, keys[block], (((1,), (1,)), ((), ())), preferred_element_type=jnp.float32
        )
        if live is not None:
            s = jnp.where(live[:, block], s, MASKED)
        scores.append(s)
    tops, sums = [], []
    for block, s in zip(blocks, scores):
        t = jnp.max(s, axis=1, keepdims=True)
        p = jnp.exp2((s - t) * SCALE2).astype(jnp.bfloat16)
        tops.append(t)
        sums.append(jnp.dot(p, values[block], preferred_element_type=jnp.float32))
    m = functools.reduce(jnp.maximum, tops)
    o = functools.reduce(
        jnp.add, [x * jnp.exp2((t - m) * SCALE2) for x, t in zip(sums, tops)]
    )
    return m, o


def kernel(
    n,
    kv,
    q_hbm,
    rk_hbm,
    rv_hbm,
    bk_hbm,
    bv_hbm,
    id_ref,
    len_ref,
    out_ref,
    qg,
    rk,
    rv,
    bk,
    bv,
    own_o,
    own_m,
    own_l,
    branch_o,
    put,
    part,
    part_l,
    recv,
    recv_l,
    done_o,
    own_sem,
    load_sem,
    qsend_sem,
    qrecv_sem,
    psend_sem,
    precv_sem,
    lsend_sem,
    lrecv_sem,
):
    me = lax.axis_index("seq")
    rows = q_hbm.shape[0]
    all_rows = n * rows
    chunks = kv * CUT
    heads = GROUP // CUT
    width = heads * HEAD_DIM
    branches = bk_hbm.shape[0]
    branch_len = bk_hbm.shape[1]
    most = 2 * rows // branches
    slots = branches * most
    has_left, has_right = me > 0, me < n - 1
    last = me == n - 1

    barrier = pltpu.get_barrier_semaphore()

    for k in range(1, REACH + 1):

        @pl.when(me >= k)
        def _():
            pl.semaphore_signal(barrier, inc=1, device_id={"seq": me - k}, device_id_type=MESH)

        @pl.when(me < n - k)
        def _():
            pl.semaphore_signal(barrier, inc=1, device_id={"seq": me + k}, device_id_type=MESH)

    def head_cols(f):
        return pl.ds(f * HEAD_DIM, HEAD_DIM)

    def shard_rows(s):
        return pl.ds(pl.multiple_of(s * rows, rows), rows)

    own = [
        pltpu.make_async_copy(
            q_hbm.at[:, pl.ds(c * width, width)], qg.at[c, shard_rows(me)], own_sem.at[c]
        )
        for c in range(chunks)
    ]
    loads, bloads = [], []
    for f in range(kv):
        loads += [
            pltpu.make_async_copy(rk_hbm.at[:, head_cols(f)], rk.at[f], load_sem.at[0, f, 0]),
            pltpu.make_async_copy(
                rv_hbm.at[:, head_cols(f)], rv.at[f, :, pl.ds(0, HEAD_DIM)], load_sem.at[1, f, 0]
            ),
        ]
        for b in range(branches):
            bloads += [
                pltpu.make_async_copy(
                    bk_hbm.at[b, :, head_cols(f)], bk.at[f, b], load_sem.at[2, f, b]
                ),
                pltpu.make_async_copy(
                    bv_hbm.at[b, :, head_cols(f)],
                    bv.at[f, b, :, pl.ds(0, HEAD_DIM)],
                    load_sem.at[3, f, b],
                ),
            ]

    def q_copy(c, s, d, slot):
        block = qg.at[c, shard_rows(s)]
        return pltpu.make_async_remote_copy(
            src_ref=block,
            dst_ref=block,
            send_sem=qsend_sem.at[c, slot],
            recv_sem=qrecv_sem.at[c, s],
            device_id={"seq": d},
            device_id_type=MESH,
        )

    def targets(do):
        for k in range(1, REACH + 1):

            @pl.when(me < n - k)
            def _():
                do(me + k, 2 * k - 2)

            @pl.when(me >= k)
            def _():
                do(me - k, 2 * k - 1)

    def send_own(c):
        targets(lambda d, slot: q_copy(c, me, d, slot).start())

    def passed(hop):
        return hop >= REACH

    def forward(t):
        for hop in range(1, n):
            c = t - hop + 1
            there = (c >= 0) & (c < chunks)
            left, right = me - hop, me + hop

            @pl.when(there & (left >= 0))
            def _():
                q_copy(c, left, me, 0).wait_recv()
                if passed(hop):

                    @pl.when(has_right)
                    def _():
                        q_copy(c, left, me + 1, 2 * hop).start()

            @pl.when(there & (right < n))
            def _():
                q_copy(c, right, me, 0).wait_recv()
                if passed(hop):

                    @pl.when(has_left)
                    def _():
                        q_copy(c, right, me - 1, 2 * hop + 1).start()

    def sent(c):
        targets(lambda d, slot: q_copy(c, me, d, slot).wait_send())
        for hop in range(REACH, n - 1):
            left, right = me - hop, me + hop

            @pl.when((left >= 0) & has_right)
            def _():
                q_copy(c, left, me + 1, 2 * hop).wait_send()

            @pl.when((right < n) & has_left)
            def _():
                q_copy(c, right, me - 1, 2 * hop + 1).wait_send()

    def greet():
        near = jnp.minimum(me, REACH) + jnp.minimum(n - 1 - me, REACH)
        pl.semaphore_wait(barrier, near)
        for c in range(chunks):
            send_own(c)

    for copy in own:
        copy.start()

    @pl.when(last)
    def _():
        for copy in own:
            copy.wait()
        greet()

    for copy in loads + bloads:
        copy.start()
    for f in range(kv):
        rv[f, :, HEAD_DIM:] = jnp.ones((rv.shape[1], HEAD_DIM), jnp.bfloat16)
        for b in range(branches):
            bv[f, b, :, HEAD_DIM:] = jnp.ones((branch_len, HEAD_DIM), jnp.bfloat16)

    slot = lax.broadcasted_iota(jnp.int32, (slots, all_rows), 0)
    named = id_ref[...] == me * branches + slot // most
    named_b = jnp.where(named, 1.0, 0.0).astype(jnp.bfloat16)
    tri = jnp.where(
        lax.broadcasted_iota(jnp.int32, (all_rows, all_rows), 0)
        <= lax.broadcasted_iota(jnp.int32, (all_rows, all_rows), 1),
        1.0,
        0.0,
    ).astype(jnp.bfloat16)
    rank = jnp.dot(named_b, tri, preferred_element_type=jnp.float32)
    pick_f = jnp.where(named & (rank == (lax.rem(slot, most) + 1).astype(jnp.float32)), 1.0, 0.0)
    pick_b = pick_f.astype(jnp.bfloat16)
    place_b = pick_f.T.astype(jnp.bfloat16)
    held = jnp.dot(
        place_b, jnp.ones((slots, HEAD_DIM), jnp.bfloat16), preferred_element_type=jnp.float32
    )

    lane = lax.broadcasted_iota(jnp.int32, (rows, HEAD_DIM), 1)
    slot_lane = lax.broadcasted_iota(jnp.int32, (slots, HEAD_DIM), 1)
    most_lane = lax.broadcasted_iota(jnp.int32, (most, HEAD_DIM), 1)
    position = lax.broadcasted_iota(jnp.int32, (1, branch_len), 1)

    def split(x, lanes):
        high = x.astype(jnp.bfloat16).astype(jnp.float32)
        rest = x - high
        mid = rest.astype(jnp.bfloat16).astype(jnp.float32)
        low = rest - mid
        return jnp.where(
            lanes < GROUP,
            high,
            jnp.where(
                lanes < 2 * GROUP, pltpu.roll(mid, GROUP, axis=1), pltpu.roll(low, 2 * GROUP, axis=1)
            ),
        ).astype(jnp.bfloat16)

    def whole(x):
        return (
            x
            + pltpu.roll(x, HEAD_DIM - GROUP, axis=1)
            + pltpu.roll(x, HEAD_DIM - 2 * GROUP, axis=1)
        )

    def p_copy(c, d, src):
        return pltpu.make_async_remote_copy(
            src_ref=part.at[c, d],
            dst_ref=recv.at[c, src],
            send_sem=psend_sem.at[c, d],
            recv_sem=precv_sem.at[c, src],
            device_id={"seq": d},
            device_id_type=MESH,
        )

    def l_copy(c, d, src):
        return pltpu.make_async_remote_copy(
            src_ref=part_l.at[c, d],
            dst_ref=recv_l.at[c, src],
            send_sem=lsend_sem.at[c, d],
            recv_sem=lrecv_sem.at[c, src],
            device_id={"seq": d},
            device_id_type=MESH,
        )

    def others(do):
        for d in range(n):

            @pl.when(me != d)
            def _(d=d):
                do(d)

    def root(f, s):
        q = jnp.concatenate(
            [qg[f, shard_rows(s), h * HEAD_DIM : (h + 1) * HEAD_DIM] for h in range(heads)],
            axis=0,
        )
        m, o = attend(q, rk[f], rv[f])
        ms = jnp.zeros((rows, HEAD_DIM), jnp.float32)
        ls = jnp.ones((rows, HEAD_DIM), jnp.float32)
        for h in range(heads):
            block = slice(h * rows, (h + 1) * rows)
            ms = jnp.where(lane == h, m[block], ms)
            ls = jnp.where(lane == h, o[block, HEAD_DIM:], ls)
        return o[:, :HEAD_DIM], ms, ls

    def root_own(f, carry):
        own_o[f], own_m[f], own_l[f] = root(f, me)
        return carry

    def branch(c):
        f = c // CUT
        picked = jnp.dot(pick_b, qg[c], preferred_element_type=jnp.float32).astype(jnp.bfloat16)
        lses = []
        for b in range(branches):
            live = position < len_ref[me * branches + b]
            mine = picked[b * most : (b + 1) * most]
            q = jnp.concatenate(
                [mine[:, h * HEAD_DIM : (h + 1) * HEAD_DIM] for h in range(heads)], axis=0
            )
            m, o = attend(q, bk[f, b], bv[f, b], live)
            ms = jnp.zeros((most, HEAD_DIM), jnp.float32)
            ls = jnp.ones((most, HEAD_DIM), jnp.float32)
            for h in range(heads):
                block = slice(h * most, (h + 1) * most)
                branch_o[b * most : (b + 1) * most, h * HEAD_DIM : (h + 1) * HEAD_DIM] = (
                    o[block, :HEAD_DIM] / o[block, HEAD_DIM:]
                ).astype(jnp.bfloat16)
                ms = jnp.where(most_lane == h, m[block], ms)
                ls = jnp.where(most_lane == h, o[block, HEAD_DIM:], ls)
            lses.append(ms * SCALE2 + jnp.log2(ls))
        branch_o[:, width:] = split(jnp.concatenate(lses, axis=0), slot_lane)
        moved = jnp.dot(place_b, branch_o[...], preferred_element_type=jnp.float32)
        put[:, :width] = moved[:, :width]
        put[:, width:] = jnp.where(held > 0.5, whole(moved[:, width:]), MASKED)

    def mix(f, d, o, ms, root_sum):
        put_s = put[shard_rows(d), width:]
        root_lse = ms * SCALE2 + jnp.log2(root_sum)
        top = jnp.maximum(root_lse, put_s)
        root_w = jnp.exp2(root_lse - top)
        branch_w = jnp.exp2(put_s - top)
        total = root_w + branch_w
        root_c = root_w / (total * root_sum)
        branch_c = branch_w / total
        part_l[f, d, :, :rows] = (top + jnp.log2(total)).T[:GROUP]
        for h in range(heads):
            cols = slice(h * HEAD_DIM, (h + 1) * HEAD_DIM)
            part[f, d, :, cols] = (
                o[h * rows : (h + 1) * rows] * root_c[:, h : h + 1]
                + put[shard_rows(d), cols] * branch_c[:, h : h + 1]
            ).astype(jnp.bfloat16)

    def finish(c, carry):
        for k in range(1, n):
            s = lax.rem(me + k, n)
            l_copy(c, me, s).wait_recv()
            p_copy(c, me, s).wait_recv()
        recv[c, me] = part[c, me]
        recv_l[c, me] = part_l[c, me]
        lse = [recv_l[c, s] for s in range(n)]
        top = functools.reduce(jnp.maximum, lse)
        weights = [jnp.exp2(x - top) for x in lse]
        total = functools.reduce(jnp.add, weights)
        coefs = [w / total for w in weights]
        spare = HEAD_DIM - n * GROUP
        if spare > 0:
            coefs.append(jnp.zeros((spare, HEAD_DIM), jnp.float32))
        coef = jnp.concatenate(coefs, axis=0).T[:rows]
        for h in range(heads):
            cols = slice(h * HEAD_DIM, (h + 1) * HEAD_DIM)
            acc = recv[c, 0, :, cols].astype(jnp.float32) * coef[:, h : h + 1]
            for s in range(1, n):
                at = s * GROUP + h
                acc += recv[c, s, :, cols].astype(jnp.float32) * coef[:, at : at + 1]
            done_o[c, :, cols] = acc.astype(jnp.bfloat16)
        pltpu.make_async_copy(done_o.at[c], out_ref.at[c], own_sem.at[c]).start()
        return carry

    @pl.when(jnp.logical_not(last))
    def _():
        for copy in own:
            copy.wait()
        greet()

    for copy in loads:
        copy.wait()
    root_own(0, 0)
    forward(0)
    if kv > 1:
        lax.fori_loop(1, kv, root_own, 0)
    lax.fori_loop(1, n - 1, lambda t, x: (forward(t), x)[1], 0)
    for copy in bloads:
        copy.wait()

    def step(f, carry):
        branch(f)

        def give(i, carry):
            d = jnp.where(i < me, i, i + 1)
            o, ms, ls = root(f, d)
            mix(f, d, o, ms, ls)
            l_copy(f, d, me).start()
            p_copy(f, d, me).start()
            return carry

        lax.fori_loop(0, n - 1, give, 0)
        forward(f + n - 1)
        mix(f, me, own_o[f], own_m[f], own_l[f])
        return carry

    lax.fori_loop(0, chunks, step, 0)
    lax.fori_loop(0, chunks, finish, 0)

    def done(c, carry):
        sent(c)

        def gone(d):
            l_copy(c, d, me).wait_send()
            p_copy(c, d, me).wait_send()

        others(gone)
        return carry

    lax.fori_loop(0, chunks, done, 0)
    for c in range(chunks):
        pltpu.make_async_copy(done_o.at[c], out_ref.at[c], own_sem.at[c]).wait()


def body(n, queries, root_keys, root_values, branch_keys, branch_values, branch_id, doc_len):
    rows = queries.shape[0]
    kv = root_keys.shape[1] // HEAD_DIM
    root_len = root_keys.shape[0]
    branches, branch_len = branch_keys.shape[:2]
    chunks = kv * CUT
    width = GROUP // CUT * HEAD_DIM
    all_rows = n * rows
    most = 2 * rows // branches
    slots = branches * most
    any_spec = pl.BlockSpec(memory_space=pl.ANY)
    bf16, f32 = jnp.bfloat16, jnp.float32
    dma = pltpu.SemaphoreType.DMA
    out = pl.pallas_call(
        functools.partial(kernel, n, kv),
        out_shape=jax.ShapeDtypeStruct((chunks, rows, width), bf16),
        in_specs=[any_spec] * 5
        + [pl.BlockSpec(memory_space=pltpu.VMEM), pl.BlockSpec(memory_space=pltpu.SMEM)],
        out_specs=any_spec,
        scratch_shapes=[
            pltpu.VMEM((chunks, all_rows, width), bf16),
            pltpu.VMEM((kv, root_len, HEAD_DIM), bf16),
            pltpu.VMEM((kv, root_len, 2 * HEAD_DIM), bf16),
            pltpu.VMEM((kv, branches, branch_len, HEAD_DIM), bf16),
            pltpu.VMEM((kv, branches, branch_len, 2 * HEAD_DIM), bf16),
            pltpu.VMEM((kv, GROUP * rows, HEAD_DIM), f32),
            pltpu.VMEM((kv, rows, HEAD_DIM), f32),
            pltpu.VMEM((kv, rows, HEAD_DIM), f32),
            pltpu.VMEM((slots, width + HEAD_DIM), bf16),
            pltpu.VMEM((all_rows, width + HEAD_DIM), f32),
            pltpu.VMEM((chunks, n, rows, width), bf16),
            pltpu.VMEM((chunks, n, GROUP, HEAD_DIM), f32),
            pltpu.VMEM((chunks, n, rows, width), bf16),
            pltpu.VMEM((chunks, n, GROUP, HEAD_DIM), f32),
            pltpu.VMEM((chunks, rows, width), bf16),
            dma((chunks,)),
            dma((4, kv, branches)),
            dma((chunks, 2 * n)),
            dma((chunks, n)),
            dma((chunks, n)),
            dma((chunks, n)),
            dma((chunks, n)),
            dma((chunks, n)),
        ],
        compiler_params=pltpu.CompilerParams(
            collective_id=0, has_side_effects=True, vmem_limit_bytes=60 * 1024 * 1024
        ),
    )(queries, root_keys, root_values, branch_keys, branch_values, branch_id.reshape(1, -1), doc_len)
    return out.transpose(1, 0, 2).reshape(queries.shape)


def solution(mesh):
    in_specs = (
        P(("parts", "seq"), "head"),
        P(("parts", "seq"), "head"),
        P(("parts", "seq"), "head"),
        P(("parts", "seq"), None, "head"),
        P(("parts", "seq"), None, "head"),
        P("parts", None),
        P("parts"),
    )
    out_specs = P(("parts", "seq"), "head")
    return jax.shard_map(
        functools.partial(body, mesh.shape["seq"]),
        mesh=mesh,
        in_specs=in_specs,
        out_specs=out_specs,
        check_vma=False,
    )
```
